32 devices in a mesh: seq: 8 (over y, x, core), tensor: 4 (over z).
Axes of the slice: x: 2, y: 2, z: 4, core: 2. Of those that a mesh axis runs over, the one named last changes fastest.
Arguments:
- block_input: bfloat16 [2048, 2048], P('seq'), may hold values from -6 to 6
- out_grad: bfloat16 [2048, 2048], P('seq'), may hold values from -6 to 6
- norm_gain: bfloat16 [2048], replicated, may hold values from 0.5 to 1.5
- norm_bias: bfloat16 [2048], replicated, may hold values from -3 to 3
- qkv_weight: bfloat16 [2048, 6144], P(None, 'tensor'), may hold values from -0.125 to 0.125
- qkv_bias: bfloat16 [6144], P('tensor'), may hold values from -3 to 3
- out_weight: bfloat16 [2048, 2048], P('tensor'), may hold values from -0.75 to 0.75
- gate_weight: bfloat16 [2048, 5632], P(None, 'tensor'), may hold values from -0.125 to 0.125
- up_weight: bfloat16 [2048, 5632], P(None, 'tensor'), may hold values from -0.125 to 0.125
- down_weight: bfloat16 [5632, 2048], P('tensor'), may hold values from -0.078125 to 0.078125
- segment_ids: int32 [2048], replicated, may hold values from 0 to 3, never falling along the last dimension, each value on 1 to 1024 neighbouring positions
- span_order: int32 [8], replicated, may hold values from 0 to 7, each once
Outputs:
- block_output: bfloat16 [2048, 2048], P('seq')
- input_grad: float32 [2048, 2048], P('seq')
- norm_gain_grad: float32 [2048], P('seq')
- norm_bias_grad: float32 [2048], P('seq')
- qkv_weight_grad: float32 [2048, 6144], P('seq', 'tensor')
- qkv_bias_grad: float32 [6144], P(('tensor', 'seq'))
- out_weight_grad: float32 [2048, 2048], P('tensor', 'seq')
- gate_weight_grad: float32 [2048, 5632], P('seq', 'tensor')
- up_weight_grad: float32 [2048, 5632], P('seq', 'tensor')
- down_weight_grad: float32 [5632, 2048], P('tensor', 'seq')
The draws below stay inside these ranges and needn't reach their ends.
Inputs may be any that keep to these rules, and one draw needn't show every extreme that they name: Token t of the row belongs to document segment_ids[t]; the ids never fall along the row, every id from 0 to 3 occurs, a document has 1 to 1024 tokens and one has exactly 1024. A permutation of 0 to 7: the device at index i of seq holds tokens span_order[i] * 256 to span_order[i] * 256 + 255 of the row.
All inputs are finite; a program needn't handle non-finite values.
Results may differ from the reference program's by a relative error of at most 0.0083.
Values may be sent and summed in bfloat16 or wider, within the bound.
No kernel may reach another device: no remote copies, remote signals or barrier semaphores. Data moves between devices by JAX's collectives and lax.ppermute only.
A program may use at most 192 MiB of HBM per device.

```python
import math
import jax
import jax.numpy as jnp
import numpy as np
from jax import lax

D = 2048
HEADS = 32
HEAD = 64
ROT = 16
FF = 5632
SEQLEN = 2048
DOCS = 4
DOC_MOST = 1024
N_SEQ = 8


def levels(rng, extent, split, smallest, largest):
    factor_of = 1.0
    for position, parts in split:
        draws = jax.random.uniform(jax.random.fold_in(jax.random.fold_in(rng, 6), position), (parts,), jnp.float32, smallest / len(split), largest / len(split))
        factor_of = factor_of * jnp.repeat(jnp.exp(draws), extent[position] // parts).reshape((-1,) + (1,) * (len(extent) - 1 - position))
    return factor_of


def profile(count, total, limit, lean):
    portions = [(1 << 20) // math.isqrt(rank ** lean) + 1 for rank in range(2, count + 1)]
    spare, counts = total - limit - (count - 1), [1] * (count - 1)
    while spare > 0:
        free = [i for i in range(count - 1) if counts[i] < limit]
        pool, left = sum([portions[i] for i in free]), spare
        for i in free:
            addition = min(limit - counts[i], max(1, left * portions[i] // pool), spare)
            counts[i] = counts[i] + addition
            spare = spare - addition
    return np.array([limit] + counts)


def uneven_parts(rng, count, total, reach, slope):
    if count == 2:
        one = jax.random.randint(rng, (), max(1, total - reach), min(reach, total - 1) + 1)
        return jnp.stack([one, total - one])
    lengths = jnp.asarray(profile(count, total, reach, slope), jnp.int32)
    couples = (count - 1) // 2
    giver, receiver = lengths[1:1 + 2 * couples:2], lengths[2:2 + 2 * couples:2]
    margin = jnp.minimum(giver - 1, reach - receiver)
    moved = jax.random.randint(jax.random.fold_in(rng, 1), (couples,), 0, 1 << 20) % (margin + 1)
    lengths = lengths.at[1:1 + 2 * couples:2].set(giver - moved).at[2:2 + 2 * couples:2].set(receiver + moved)
    return lengths[jax.random.permutation(jax.random.fold_in(rng, 2), count)]


def normal_values(rng, shape, spread, limit, cuts=(), kind=jnp.bfloat16):
    loudness = levels(rng, shape, cuts, -0.22, 0.18) if cuts else 1.0
    drawn = jax.random.normal(rng, shape, jnp.float32) * spread * loudness
    return jnp.minimum(jnp.maximum(drawn, -limit), limit).astype(kind)


def setup_inputs(seed: int = 0) -> dict:
    key_list = jax.random.split(jax.random.key(seed), 13)
    return {
        "block_input": normal_values(key_list[0], (SEQLEN, D), 1.0, 6.0, ((0, 8),)),
        "out_grad": normal_values(key_list[1], (SEQLEN, D), 1.0, 6.0, ((0, 8),)),
        "norm_gain": jnp.clip(1.0 + 0.1 * jax.random.normal(key_list[2], (D,), jnp.float32), 0.5, 1.5).astype(jnp.bfloat16),
        "norm_bias": normal_values(key_list[3], (D,), 0.5, 3.0),
        "qkv_weight": normal_values(key_list[4], (D, 3 * D), D ** -0.5, 0.125, ((1, 4),)),
        "qkv_bias": normal_values(key_list[5], (3 * D,), 0.5, 3.0, ((0, 4),)),
        "out_weight": normal_values(key_list[6], (D, D), (max(D // 32, 16)) ** -0.5, 0.75, ((0, 4),)),
        "gate_weight": normal_values(key_list[7], (D, FF), D ** -0.5, 0.125, ((1, 4),)),
        "up_weight": normal_values(key_list[8], (D, FF), D ** -0.5, 0.125, ((1, 4),)),
        "down_weight": normal_values(key_list[9], (FF, D), FF ** -0.5, 0.078125, ((0, 4),)),
        "segment_ids": jnp.searchsorted(jnp.cumsum(uneven_parts(key_list[10], DOCS, SEQLEN, DOC_MOST, 1)), jnp.arange(SEQLEN), side="right").astype(jnp.int32),
        "span_order": jax.random.permutation(key_list[11], N_SEQ).astype(jnp.int32),
    }


@jax.custom_vjp
def low(v):
    return lax.optimization_barrier(v.astype(jnp.bfloat16)).astype(jnp.float32)

@jax.custom_vjp
def low_back(v):
    return v

def low_keep(v):
    return (low(v), None)

def low_pass(kept, grad):
    return (grad,)

def back_keep(v):
    return (v, None)

def back_low(kept, grad):
    return (low(grad),)
low.defvjp(low_keep, low_pass)
low_back.defvjp(back_keep, back_low)
epsilon = 1e-05
masked_value = 1e+30

def doc_positions(segment_ids):
    count_all = segment_ids.shape[0]
    token_index = jnp.arange(count_all, dtype=jnp.int32)
    earlier = jnp.concatenate([segment_ids[:1] - 1, segment_ids[:-1]])
    starts = jnp.where(segment_ids != earlier, token_index, 0)
    return token_index - lax.cummax(starts, axis=0)

def rope_tables(positions, rot_dims):
    half_rot = rot_dims // 2
    frequency = jnp.exp(jnp.arange(half_rot, dtype=jnp.float32) * (-2.0 * math.log(10000.0) / rot_dims))
    angles = positions.astype(jnp.float32)[:, None] * frequency[None, :]
    return (jnp.cos(angles)[:, None, :], jnp.sin(angles)[:, None, :])

def rotate(values_in, cosine, sine, rot_dims):
    half_rot = rot_dims // 2
    first_half = values_in[..., :half_rot]
    second_half = values_in[..., half_rot:rot_dims]
    return jnp.concatenate([first_half * cosine - second_half * sine, second_half * cosine + first_half * sine, values_in[..., rot_dims:]], axis=-1)

def matmul(left_side, right_side):
    return jnp.dot(left_side, right_side, precision=lax.Precision.HIGHEST, preferred_element_type=jnp.float32)

def reference(block_input, out_grad, norm_gain, norm_bias, qkv_weight, qkv_bias, out_weight, gate_weight, up_weight, down_weight, segment_ids, span_order):
    seq_devices = span_order.shape[0]
    row_tokens = segment_ids.shape[0]
    span_rows = row_tokens // seq_devices
    inverse = jnp.zeros((seq_devices,), jnp.int32).at[span_order].set(jnp.arange(seq_devices, dtype=jnp.int32))

    def to_rows(matrix):
        return matrix.reshape(seq_devices, span_rows, matrix.shape[-1])[inverse].reshape(row_tokens, matrix.shape[-1])

    def to_devices(matrix):
        return matrix.reshape(seq_devices, span_rows, matrix.shape[-1])[span_order].reshape(row_tokens, matrix.shape[-1])
    token_index = jnp.arange(row_tokens, dtype=jnp.int32)
    cosine, sine = rope_tables(doc_positions(segment_ids), ROT)
    block_rows = min(256, row_tokens)
    block_count = row_tokens // block_rows
    score_scale = HEAD ** (-0.5)

    def forward(inputs, gain, shift, w_qkv, b_qkv, w_out, w_gate, w_up, w_down):
        row_mean = lax.optimization_barrier(jnp.mean(inputs, axis=-1, keepdims=True))
        centered = inputs - row_mean
        row_var = lax.optimization_barrier(jnp.mean(centered * centered, axis=-1, keepdims=True))
        normed = low(centered * lax.rsqrt(row_var + epsilon) * gain + shift)
        mixed = low_back(matmul(normed, w_qkv) + b_qkv).reshape(row_tokens, HEADS, 3, HEAD)
        queries = low(rotate(mixed[:, :, 0], cosine, sine, ROT))
        keys_all = low(rotate(mixed[:, :, 1], cosine, sine, ROT))
        values_all = low(mixed[:, :, 2])

        def attend(pieces):
            query_block, query_index, query_segs = pieces
            raw_scores = jnp.einsum('qhd,khd->hqk', query_block, keys_all, precision=lax.Precision.HIGHEST)
            scores = low_back(raw_scores * score_scale)
            allowed_pairs = (token_index[None, :] <= query_index[:, None]) & (segment_ids[None, :] == query_segs[:, None])
            scores = jnp.where(allowed_pairs[None], scores, -masked_value)
            row_top = lax.optimization_barrier(jnp.max(scores, axis=-1, keepdims=True))
            expo = jnp.exp(scores - row_top)
            probability = expo / lax.optimization_barrier(jnp.sum(expo, axis=-1, keepdims=True))
            return jnp.einsum('hqk,khd->qhd', low(probability), values_all, precision=lax.Precision.HIGHEST)
        attended = lax.map(jax.checkpoint(attend), (queries.reshape(block_count, block_rows, HEADS, HEAD), token_index.reshape(block_count, block_rows), segment_ids.reshape(block_count, block_rows)))
        attended = low(low_back(attended.reshape(row_tokens, D)))
        gate_proj = low_back(matmul(normed, w_gate))
        up_proj = low_back(matmul(normed, w_up))
        hidden = low(gate_proj * jax.nn.sigmoid(gate_proj) * up_proj)
        return inputs + matmul(attended, w_out) + matmul(hidden, w_down)
    inputs = (to_rows(block_input.astype(jnp.float32)), norm_gain.astype(jnp.float32), norm_bias.astype(jnp.float32), qkv_weight.astype(jnp.float32), qkv_bias.astype(jnp.float32), out_weight.astype(jnp.float32), gate_weight.astype(jnp.float32), up_weight.astype(jnp.float32), down_weight.astype(jnp.float32))
    output, pullback = jax.vjp(forward, *inputs)
    grads = pullback(to_rows(out_grad.astype(jnp.float32)))
    return (to_devices(output).astype(jnp.bfloat16), to_devices(grads[0]), grads[1], grads[2], grads[3], grads[4], grads[5], grads[6], grads[7], grads[8])
```

```python
import functools
import math

import jax
import jax.numpy as jnp
from jax import lax
from jax.experimental import pallas as pl
from jax.experimental.pallas import tpu as pltpu
from jax.sharding import PartitionSpec as P

HEAD = 64
ROT = 16


epsilon = 1e-05
masked_value = 1e30


def doc_positions(segment_ids):
    count_all = segment_ids.shape[0]
    token_index = jnp.arange(count_all, dtype=jnp.int32)
    earlier = jnp.concatenate([segment_ids[:1] - 1, segment_ids[:-1]])
    starts = jnp.where(segment_ids != earlier, token_index, 0)
    return token_index - lax.cummax(starts, axis=0)


def rope_tables(positions, rot_dims):
    half_rot = rot_dims // 2
    frequency = jnp.exp(
        jnp.arange(half_rot, dtype=jnp.float32) * (-2.0 * math.log(10000.0) / rot_dims)
    )
    angles = positions.astype(jnp.float32)[:, None] * frequency[None, :]
    return (jnp.cos(angles)[:, None, :], jnp.sin(angles)[:, None, :])


def rotate(values_in, cosine, sine, rot_dims):
    half_rot = rot_dims // 2
    first_half = values_in[..., :half_rot]
    second_half = values_in[..., half_rot:rot_dims]
    return jnp.concatenate(
        [
            first_half * cosine - second_half * sine,
            second_half * cosine + first_half * sine,
            values_in[..., rot_dims:],
        ],
        axis=-1,
    )


def unrotate(incoming, cosine, sine, rot_dims):
    half_rot = rot_dims // 2
    first_half = incoming[..., :half_rot]
    second_half = incoming[..., half_rot:rot_dims]
    return jnp.concatenate(
        [
            first_half * cosine + second_half * sine,
            second_half * cosine - first_half * sine,
            incoming[..., rot_dims:],
        ],
        axis=-1,
    )


def lookup(small_table, position):
    return jnp.sum(
        jnp.where(jnp.arange(small_table.shape[0], dtype=jnp.int32) == position, small_table, 0)
    )


def inner(left_side, right_side):
    return lax.dot_general(
        left_side, right_side, (((0,), (0,)), ((), ())), preferred_element_type=jnp.float32
    )


def outer_t(left_side, right_side):
    return lax.dot_general(
        left_side, right_side, (((1,), (1,)), ((), ())), preferred_element_type=jnp.float32
    )


def allowed(query_tokens, query_segs, key_tokens, key_segs):
    return (key_tokens[None, :] <= query_tokens[:, None]) & (
        key_segs[None, :] == query_segs[:, None]
    )


def score_block(query_block, key_block, allowed_pairs, score_scale):
    raw_scores = jnp.einsum(
        "qhd,khd->hqk", query_block, key_block, preferred_element_type=jnp.float32
    )
    return jnp.where(allowed_pairs[None], raw_scores * score_scale, -masked_value)


def norm_back(d_normed, normal, inv_dev, gain):
    d_normal = d_normed * gain
    return inv_dev * (
        d_normal
        - jnp.mean(d_normal, axis=-1, keepdims=True)
        - normal * jnp.mean(d_normal * normal, axis=-1, keepdims=True)
    )


def local(
    block_input,
    out_grad,
    norm_gain,
    norm_bias,
    qkv_weight,
    qkv_bias,
    out_weight,
    gate_weight,
    up_weight,
    down_weight,
    segment_ids,
    span_order,
):
    span_rows, width = block_input.shape
    seq_devices = lax.axis_size("seq")
    row_tokens = span_rows * seq_devices
    head_dim = HEAD
    rot_dims = ROT
    heads_local = qkv_weight.shape[1] // (3 * head_dim)
    local_width = heads_local * head_dim
    score_scale = head_dim ** (-0.5)
    block_rows = min(1024, span_rows)
    key_blocks = row_tokens // block_rows
    block_ids = jnp.arange(key_blocks, dtype=jnp.int32)
    own_span = lookup(span_order, lax.axis_index("seq"))
    first_row = own_span * span_rows
    last_row = first_row + span_rows - 1
    own_tokens = first_row + jnp.arange(span_rows, dtype=jnp.int32)
    own_segs = lax.dynamic_slice_in_dim(segment_ids, first_row, span_rows)
    positions = lax.dynamic_slice_in_dim(doc_positions(segment_ids), first_row, span_rows)
    cosine, sine = rope_tables(positions, rot_dims)

    def seg_at(position):
        return lax.dynamic_index_in_dim(segment_ids, position, keepdims=False)

    own_seg_first = seg_at(first_row)

    def geometry(block_index):
        row_start = block_index * block_rows
        token_start = lookup(span_order, row_start // span_rows) * span_rows + row_start % span_rows
        tokens_here = token_start + jnp.arange(block_rows, dtype=jnp.int32)
        return (
            row_start,
            token_start,
            tokens_here,
            lax.dynamic_slice_in_dim(segment_ids, token_start, block_rows),
        )

    def key_live(token_start):
        return (token_start <= last_row) & (seg_at(token_start + block_rows - 1) >= own_seg_first)

    inputs_f32 = block_input.astype(jnp.float32)
    row_mean = jnp.mean(inputs_f32, axis=-1, keepdims=True)
    centered = inputs_f32 - row_mean
    row_var = jnp.mean(centered * centered, axis=-1, keepdims=True)
    inv_dev = lax.rsqrt(row_var + epsilon)
    normal = centered * inv_dev
    gain_f32 = norm_gain.astype(jnp.float32)
    normed = (normal * gain_f32 + norm_bias.astype(jnp.float32)).astype(jnp.bfloat16)
    mixed = (
        jnp.dot(normed, qkv_weight, preferred_element_type=jnp.float32)
        + qkv_bias.astype(jnp.float32)
    ).reshape(span_rows, heads_local, 3, head_dim)
    query_own = rotate(mixed[:, :, 0], cosine, sine, rot_dims).astype(jnp.bfloat16)
    key_own = rotate(mixed[:, :, 1], cosine, sine, rot_dims).astype(jnp.bfloat16)
    value_own = mixed[:, :, 2].astype(jnp.bfloat16)
    d_out = (
        outer_t(out_grad, out_weight).astype(jnp.bfloat16).reshape(span_rows, heads_local, head_dim)
    )
    key_all, value_all = (
        lax.all_gather(key_own.reshape(span_rows, local_width), "seq", axis=0, tiled=True),
        lax.all_gather(value_own.reshape(span_rows, local_width), "seq", axis=0, tiled=True),
    )

    def key_slices(row_start):
        key_block = lax.dynamic_slice_in_dim(key_all, row_start, block_rows, 0).reshape(
            block_rows, heads_local, head_dim
        )
        value_block = lax.dynamic_slice_in_dim(value_all, row_start, block_rows, 0).reshape(
            block_rows, heads_local, head_dim
        )
        return (key_block, value_block)

    def first_pass(running, block_index):
        row_start, token_start, tokens_here, segs_here = geometry(block_index)

        def first_visit_block(state_in):
            row_top, row_sums = state_in
            key_block, value_block = key_slices(row_start)
            scores = score_block(
                query_own,
                key_block,
                allowed(own_tokens, own_segs, tokens_here, segs_here),
                score_scale,
            )
            new_top = jnp.maximum(row_top, jnp.max(scores, axis=-1))
            row_sums = row_sums * jnp.exp(row_top - new_top) + jnp.sum(
                jnp.exp(scores - new_top[..., None]), axis=-1
            )
            return (new_top, row_sums)

        def first_skip_block(state_in):
            return state_in

        return (lax.cond(key_live(token_start), first_visit_block, first_skip_block, running), None)

    start_top = jnp.full((heads_local, span_rows), -masked_value, jnp.float32)
    start_sums = jnp.zeros((heads_local, span_rows), jnp.float32)
    (row_top, row_sums), unused = lax.scan(first_pass, (start_top, start_sums), block_ids)
    log_total = row_top + jnp.log(row_sums)

    def second_pass(running, block_index):
        row_start, token_start, tokens_here, segs_here = geometry(block_index)

        def second_visit_block(state_in):
            attended, prob_dots = state_in
            key_block, value_block = key_slices(row_start)
            scores = score_block(
                query_own,
                key_block,
                allowed(own_tokens, own_segs, tokens_here, segs_here),
                score_scale,
            )
            probability = jnp.exp(scores - log_total[..., None])
            attended = attended + jnp.einsum(
                "hqk,khd->qhd",
                probability.astype(jnp.bfloat16),
                value_block,
                preferred_element_type=jnp.float32,
            )
            grad_prob = jnp.einsum(
                "qhd,khd->hqk", d_out, value_block, preferred_element_type=jnp.float32
            )
            return (attended, prob_dots + jnp.sum(probability * grad_prob, axis=-1))

        def second_skip_block(state_in):
            return state_in

        return (
            lax.cond(key_live(token_start), second_visit_block, second_skip_block, running),
            None,
        )

    start_out = jnp.zeros((span_rows, heads_local, head_dim), jnp.float32)
    (attended, prob_dots), unused = lax.scan(second_pass, (start_out, start_sums), block_ids)
    attended_low = attended.astype(jnp.bfloat16).reshape(span_rows, local_width)
    gate_proj = jnp.dot(normed, gate_weight, preferred_element_type=jnp.float32)
    up_proj = jnp.dot(normed, up_weight, preferred_element_type=jnp.float32)
    gate_sigmoid = jax.nn.sigmoid(gate_proj)
    hidden_low = (gate_proj * gate_sigmoid * up_proj).astype(jnp.bfloat16)
    partial_out = jnp.dot(attended_low, out_weight, preferred_element_type=jnp.float32) + jnp.dot(
        hidden_low, down_weight, preferred_element_type=jnp.float32
    )
    block_output = (inputs_f32 + lax.psum(partial_out, "tensor")).astype(jnp.bfloat16)
    d_hidden = outer_t(out_grad, down_weight)
    d_gate = (
        d_hidden * up_proj * (gate_sigmoid * (1.0 + gate_proj * (1.0 - gate_sigmoid)))
    ).astype(jnp.bfloat16)
    d_up = (d_hidden * gate_proj * gate_sigmoid).astype(jnp.bfloat16)

    def query_side():

        def step_block(running, block_index):
            row_start, token_start, tokens_here, segs_here = geometry(block_index)

            def step_visit_block(grad_query):
                key_block, value_block = key_slices(row_start)
                scores = score_block(
                    query_own,
                    key_block,
                    allowed(own_tokens, own_segs, tokens_here, segs_here),
                    score_scale,
                )
                probability = jnp.exp(scores - log_total[..., None])
                grad_prob = jnp.einsum(
                    "qhd,khd->hqk", d_out, value_block, preferred_element_type=jnp.float32
                )
                grad_score = (probability * (grad_prob - prob_dots[..., None])).astype(jnp.bfloat16)
                grad_query = grad_query + score_scale * jnp.einsum(
                    "hqk,khd->qhd", grad_score, key_block, preferred_element_type=jnp.float32
                )
                key_grad = score_scale * jnp.einsum(
                    "hqk,qhd->khd", grad_score, query_own, preferred_element_type=jnp.float32
                )
                value_grad = jnp.einsum(
                    "hqk,qhd->khd",
                    probability.astype(jnp.bfloat16),
                    d_out,
                    preferred_element_type=jnp.float32,
                )
                return (
                    grad_query,
                    (
                        key_grad.reshape(block_rows, local_width),
                        value_grad.reshape(block_rows, local_width),
                    ),
                )

            def step_skip_block(grad_query):
                nothing = jnp.zeros((block_rows, local_width), jnp.float32)
                return (grad_query, (nothing, nothing))

            return lax.cond(key_live(token_start), step_visit_block, step_skip_block, running)

        return step_block

    grad_query, key_terms = lax.scan(query_side(), start_out, block_ids)
    key_grad_all = key_terms[0].reshape(row_tokens, local_width)
    value_grad_all = key_terms[1].reshape(row_tokens, local_width)
    grad_key, grad_value = (
        lax.psum_scatter(key_grad_all, "seq", scatter_dimension=0, tiled=True),
        lax.psum_scatter(value_grad_all, "seq", scatter_dimension=0, tiled=True),
    )
    grad_key = grad_key.reshape(span_rows, heads_local, head_dim)
    grad_value = grad_value.reshape(span_rows, heads_local, head_dim)
    d_mixed = jnp.stack(
        [
            unrotate(grad_query, cosine, sine, rot_dims),
            unrotate(grad_key, cosine, sine, rot_dims),
            grad_value,
        ],
        axis=2,
    )
    d_mixed = d_mixed.reshape(span_rows, 3 * local_width).astype(jnp.bfloat16)
    qkv_grad = inner(normed, d_mixed)
    qkv_bias_grad = jnp.sum(d_mixed.astype(jnp.float32), axis=0)
    w_out_grad = inner(attended_low, out_grad)
    gate_grad = inner(normed, d_gate)
    up_grad = inner(normed, d_up)
    down_grad = inner(hidden_low, out_grad)
    d_partial = (
        outer_t(d_mixed, qkv_weight) + outer_t(d_gate, gate_weight) + outer_t(d_up, up_weight)
    )
    cotangent = out_grad.astype(jnp.float32)
    d_normed = lax.psum(d_partial, "tensor")
    input_grad = cotangent + norm_back(d_normed, normal, inv_dev, gain_f32)
    gain_grad = jnp.sum(d_normed * normal, axis=0)
    bias_grad = jnp.sum(d_normed, axis=0)
    reduced = (
        lax.psum_scatter(gain_grad, "seq", scatter_dimension=0, tiled=True),
        lax.psum_scatter(bias_grad, "seq", scatter_dimension=0, tiled=True),
        lax.psum_scatter(qkv_grad, "seq", scatter_dimension=0, tiled=True),
        lax.psum_scatter(qkv_bias_grad, "seq", scatter_dimension=0, tiled=True),
        lax.psum_scatter(w_out_grad, "seq", scatter_dimension=1, tiled=True),
        lax.psum_scatter(gate_grad, "seq", scatter_dimension=0, tiled=True),
        lax.psum_scatter(up_grad, "seq", scatter_dimension=0, tiled=True),
        lax.psum_scatter(down_grad, "seq", scatter_dimension=1, tiled=True),
    )
    return (
        block_output,
        input_grad,
        reduced[0],
        reduced[1],
        reduced[2],
        reduced[3],
        reduced[4],
        reduced[5],
        reduced[6],
        reduced[7],
    )


F32 = jnp.float32
BF16 = jnp.bfloat16


def mm(left_side, right_side):
    return lax.dot_general(
        left_side, right_side, (((1,), (0,)), ((), ())), preferred_element_type=F32
    )


def attention_body(
    place_ref,
    slot_ref,
    low_ref,
    in0,
    in1,
    in2,
    in3,
    start_ref,
    turn_ref,
    out_ref,
    q_s,
    k_s,
    v_s,
    g_s,
    o_s,
    dq_s,
    dk_s,
    dv_s,
    s_s,
    p_s,
):
    blocks = place_ref.shape[0]
    rows = in0.shape[0] // 2
    head_dim = in0.shape[1] // 4
    scale = head_dim ** (-0.5)
    for n in range(blocks):
        at = pl.ds(pl.multiple_of(place_ref[n] * rows, rows), rows)
        piece = (in0, in1, in2, in3)[n // 2][(n % 2) * rows : (n % 2 + 1) * rows, :]
        q_s[at, :] = (piece[:, :head_dim].astype(F32) * scale).astype(BF16)
        k_s[at, :] = piece[:, head_dim : 2 * head_dim]
        v_s[at, :] = piece[:, 2 * head_dim : 3 * head_dim]
        g_s[at, :] = piece[:, 3 * head_dim :]
    dk_s[...] = jnp.zeros_like(dk_s)
    dv_s[...] = jnp.zeros_like(dv_s)

    def fold(block):
        return functools.reduce(
            jnp.add, [block[:, a : a + 128] for a in range(0, rows, 128)]
        )

    def turn_back(values_in, at):
        lane = lax.broadcasted_iota(jnp.int32, values_in.shape, 1)
        other = jnp.where(
            lane < ROT // 2,
            jnp.roll(values_in, -(ROT // 2), 1),
            jnp.roll(values_in, ROT // 2, 1),
        )
        table = turn_ref[at, :]
        return values_in * table[:, :head_dim] + other * table[:, head_dim:]

    def query_block(i, unused):
        at = pl.ds(pl.multiple_of(i * rows, rows), rows)
        q_i, g_i = q_s[at, :], g_s[at, :]
        start = start_ref[at, :]
        row = i * rows + lax.broadcasted_iota(jnp.int32, (rows, rows), 0)
        column = lax.broadcasted_iota(jnp.int32, (rows, rows), 1)

        def here(j):
            return pl.ds(pl.multiple_of(j * rows, rows), rows)

        def scores(j, top):
            s = outer_t(q_i, k_s[here(j), :])
            col = j * rows + column
            s = jnp.where((col <= row) & (col >= start), s, -masked_value)
            s_s[j] = s
            for a in range(0, rows, 128):
                top = jnp.maximum(top, s[:, a : a + 128])
            return top

        top = lax.fori_loop(
            low_ref[i], i + 1, scores, jnp.full((rows, 128), -masked_value, F32)
        )
        top = jnp.max(top, axis=1, keepdims=True)

        def weigh(j, sums):
            total, dots = sums
            e = jnp.exp(s_s[j] - top)
            s_s[j] = e
            d = outer_t(g_i, v_s[here(j), :])
            p_s[j] = d
            return total + fold(e), dots + fold(e * d)

        nothing = jnp.zeros((rows, 128), F32)
        total, dots = lax.fori_loop(low_ref[i], i + 1, weigh, (nothing, nothing))
        total = jnp.sum(total, axis=1, keepdims=True)
        shrink = 1.0 / total
        delta = jnp.sum(dots, axis=1, keepdims=True) * shrink

        def gather(j, sums):
            o, dq = sums
            at_j = here(j)
            p = s_s[j] * shrink
            ds = (p * (p_s[j] - delta)).astype(BF16)
            p = p.astype(BF16)
            dk_s[at_j, :] += inner(ds, q_i)
            dv_s[at_j, :] += inner(p, g_i)
            return o + mm(p, v_s[at_j, :]), dq + mm(ds, k_s[at_j, :])

        empty = jnp.zeros((rows, head_dim), F32)
        o, dq = lax.fori_loop(low_ref[i], i + 1, gather, (empty, empty))
        o_s[at, :] = o
        dq_s[at, :] = turn_back(dq * scale, at)
        return unused

    lax.fori_loop(0, blocks, query_block, 0)

    def finish(i, unused):
        at = pl.ds(pl.multiple_of(i * rows, rows), rows)
        out_ref[slot_ref[i]] = jnp.concatenate(
            [dq_s[at, :], turn_back(dk_s[at, :], at), dv_s[at, :], o_s[at, :]], axis=1
        ).astype(BF16)
        return unused

    lax.fori_loop(0, blocks, finish, 0)


def attention(place, slot, low, pieces, start, turn):
    blocks = place.shape[0]
    rows, lanes = pieces[0].shape[0] // 2, pieces[0].shape[1]
    head_dim = lanes // 4
    tokens = blocks * rows
    smem = pl.BlockSpec(memory_space=pltpu.SMEM)
    vmem = pl.BlockSpec(memory_space=pltpu.VMEM)
    low_kind = pltpu.VMEM((tokens, head_dim), BF16)
    full_kind = pltpu.VMEM((tokens, head_dim), F32)
    return pl.pallas_call(
        attention_body,
        out_shape=jax.ShapeDtypeStruct((blocks, rows, lanes), BF16),
        in_specs=[smem] * 3 + [vmem] * 6,
        out_specs=vmem,
        scratch_shapes=[low_kind] * 4
        + [full_kind] * 4
        + [pltpu.VMEM((blocks, rows, rows), F32)] * 2,
        compiler_params=pltpu.CompilerParams(vmem_limit_bytes=32 * 1024 * 1024),
        cost_estimate=pl.CostEstimate(
            flops=12 * tokens * tokens * head_dim // 2,
            bytes_accessed=8 * tokens * lanes,
            transcendentals=tokens * tokens // 2,
        ),
        name="attention",
    )(place, slot, low, *pieces, start, turn)


def paired(
    block_input,
    out_grad,
    norm_gain,
    norm_bias,
    qkv_weight,
    qkv_bias,
    out_weight,
    gate_weight,
    up_weight,
    down_weight,
    segment_ids,
    span_order,
):
    span_rows, width = block_input.shape
    row_tokens = segment_ids.shape[0]
    tensor_devices = lax.axis_size("tensor")
    devices = lax.axis_size("seq")
    head_dim = HEAD
    heads = qkv_weight.shape[1] // (3 * head_dim)
    half_heads = heads // 2
    hidden = gate_weight.shape[1]
    half_hidden = -(-hidden // 256) * 128
    skip_hidden = hidden - half_hidden
    me = lax.axis_index("seq")
    core = me & 1
    chip = me >> 1
    gather_bit = 1 << core
    reduce_bit = 2 >> core
    slab = 2 * span_rows

    def swap(values_in, bits):
        return lax.ppermute(values_in, "seq", [(i, i ^ bits) for i in range(devices)])

    def gather_swap(values_in):
        return lax.ppermute(
            values_in, "seq", [(i, i ^ (2 << (i & 1))) for i in range(devices)]
        )

    def reduce_swap(values_in):
        return lax.ppermute(
            values_in, "seq", [(i, i ^ (4 >> (i & 1))) for i in range(devices)]
        )

    positions_all = doc_positions(segment_ids)
    token_index = jnp.arange(row_tokens, dtype=jnp.int32)
    start = (token_index - positions_all)[:, None]
    low = (token_index - positions_all)[::span_rows] // span_rows
    slots = jnp.arange(devices, dtype=jnp.int32)
    slot_device = 2 * (chip ^ (slots >> 1)) + ((slots & 1) ^ core)
    place = jnp.sum(
        jnp.where(slot_device[:, None] == slots[None, :], span_order[None, :], 0), axis=1
    )
    slot = jnp.sum(jnp.where(place[None, :] == slots[:, None], slots[None, :], 0), axis=1)
    half_rot = ROT // 2
    frequency = jnp.exp(
        jnp.arange(half_rot, dtype=F32) * (-2.0 * math.log(10000.0) / ROT)
    )
    angles = frequency[:, None] * positions_all.astype(F32)[None, :]
    cosine, sine = jnp.cos(angles).T, jnp.sin(angles).T
    passing = head_dim - ROT
    turn = jnp.concatenate(
        [
            cosine,
            cosine,
            jnp.ones((row_tokens, passing), F32),
            sine,
            -sine,
            jnp.zeros((row_tokens, passing), F32),
        ],
        axis=1,
    )

    def own(table, device):
        return lax.dynamic_slice_in_dim(
            table, lookup(span_order, device) * span_rows, span_rows
        )

    turn_chip = jnp.concatenate([own(turn, me), own(turn, me ^ 1)], axis=0)

    inputs_f32 = block_input.astype(F32)
    row_mean = jnp.mean(inputs_f32, axis=-1, keepdims=True)
    centered = inputs_f32 - row_mean
    row_var = jnp.mean(centered * centered, axis=-1, keepdims=True)
    inv_dev = lax.rsqrt(row_var + epsilon)
    normal = centered * inv_dev
    gain_f32 = norm_gain.astype(F32)
    normed = (normal * gain_f32 + norm_bias.astype(F32)).astype(BF16)

    grad_chip = jnp.concatenate([out_grad, swap(out_grad, 1)], axis=0)
    normed_chip = jnp.concatenate([normed, swap(normed, 1)], axis=0)
    grad_far = gather_swap(grad_chip)
    normed_far = gather_swap(normed_chip)

    wide = half_heads * 3 * head_dim
    w_qkv = lax.dynamic_slice_in_dim(qkv_weight, core * wide, wide, 1)
    b_qkv = lax.dynamic_slice_in_dim(qkv_bias, core * wide, wide, 0)
    w_out = lax.dynamic_slice_in_dim(out_weight, core * half_heads * head_dim, half_heads * head_dim, 0)
    mixed = (mm(normed_chip, w_qkv) + b_qkv.astype(F32)).reshape(
        slab, half_heads, 3, head_dim
    )
    cos_chip = turn_chip[:, None, :half_rot]
    sin_chip = turn_chip[:, None, head_dim : head_dim + half_rot]
    d_out = outer_t(grad_chip, w_out).astype(BF16).reshape(slab, half_heads, head_dim)
    packed = jnp.concatenate(
        [
            rotate(mixed[:, :, 0], cos_chip, sin_chip, ROT).astype(BF16),
            rotate(mixed[:, :, 1], cos_chip, sin_chip, ROT).astype(BF16),
            mixed[:, :, 2].astype(BF16),
            d_out,
        ],
        axis=-1,
    ).transpose(1, 0, 2)

    def head_of(values_in, r):
        return lax.dynamic_index_in_dim(values_in, chip ^ r, 0, keepdims=False)

    pieces = [head_of(packed, 0)] + [swap(head_of(packed, r), 2 * r) for r in (1, 2, 3)]
    done = attention(place, slot, low, pieces, start, turn)
    bias_sum = jnp.sum(done[:, :, : 3 * head_dim].astype(F32), axis=(0, 1))
    qkv_bias_grad = lax.ppermute(
        bias_sum,
        "seq",
        [(i, (i & 1) * half_heads + (i >> 1)) for i in range(devices)],
    )
    back = [done[0:2].reshape(slab, 4 * head_dim)] + [
        swap(done[2 * r : 2 * r + 2].reshape(slab, 4 * head_dim), 2 * r) for r in (1, 2, 3)
    ]
    back = jnp.stack(back)
    back_far = gather_swap(back)
    back_other = swap(back[:, span_rows:], 1)

    def ordered(values_in, base):
        return jnp.stack([lax.dynamic_index_in_dim(values_in, base ^ k, 0, False) for k in range(4)])

    def heads_flat(values_in, first, last):
        return (
            values_in[:, :, first:last]
            .transpose(1, 0, 2)
            .reshape(values_in.shape[1], values_in.shape[0] * (last - first))
        )

    mine = ordered(back, chip)
    far = ordered(back_far, chip ^ gather_bit)
    mine_own = mine[:, :span_rows]
    other = ordered(back_other, chip)
    d_mixed_half = jnp.concatenate(
        [heads_flat(mine, 0, 3 * head_dim), heads_flat(far, 0, 3 * head_dim)], axis=0
    )
    attended_half = jnp.concatenate(
        [heads_flat(mine, 3 * head_dim, 4 * head_dim), heads_flat(far, 3 * head_dim, 4 * head_dim)],
        axis=0,
    )
    first = jnp.where(core == 0, mine_own, other)
    second = jnp.where(core == 0, other, mine_own)
    all_heads = jnp.concatenate([first, second], axis=0)
    d_mixed = heads_flat(all_heads, 0, 3 * head_dim)
    attended_low = heads_flat(all_heads, 3 * head_dim, 4 * head_dim)

    w_gate = lax.dynamic_slice_in_dim(gate_weight, core * skip_hidden, half_hidden, 1)
    w_up = lax.dynamic_slice_in_dim(up_weight, core * skip_hidden, half_hidden, 1)
    w_down = lax.dynamic_slice_in_dim(down_weight, core * skip_hidden, half_hidden, 0)

    def feed(tokens_normed, tokens_grad):
        gate_proj = mm(tokens_normed, w_gate)
        up_proj = mm(tokens_normed, w_up)
        d_hidden = outer_t(tokens_grad, w_down)
        gate_sigmoid = jax.nn.sigmoid(gate_proj)
        hidden_low = (gate_proj * gate_sigmoid * up_proj).astype(BF16)
        d_gate = (
            d_hidden * up_proj * (gate_sigmoid * (1.0 + gate_proj * (1.0 - gate_sigmoid)))
        ).astype(BF16)
        d_up = (d_hidden * gate_proj * gate_sigmoid).astype(BF16)
        return hidden_low, d_gate, d_up

    feed_chip = feed(normed_chip, grad_chip)
    feed_far = feed(normed_far, grad_far)
    hidden_half, d_gate_half, d_up_half = (
        jnp.concatenate([near, away], axis=0) for near, away in zip(feed_chip, feed_far)
    )

    def whole(mine_half, other_half, axis):
        lo = jnp.where(core == 0, mine_half, other_half)
        hi = jnp.where(core == 0, other_half, mine_half)
        hi = lax.slice_in_dim(hi, half_hidden - skip_hidden, half_hidden, axis=axis)
        return jnp.concatenate([lo, hi], axis=axis)

    shared = [swap(near[span_rows:], 1) for near in feed_chip]
    hidden_low, d_gate, d_up = (
        whole(near[:span_rows], got, 1) for near, got in zip(feed_chip, shared)
    )

    third = lax.axis_index("tensor")

    def tensor_swap(values_in, bit):
        return lax.ppermute(
            values_in, "tensor", [(i, i ^ bit) for i in range(tensor_devices)]
        )

    def share_sum(values_in):
        bit, count = 1, values_in.shape[0]
        while bit < tensor_devices:
            count //= 2
            up = (third // bit) & 1
            keep = lax.dynamic_slice_in_dim(values_in, up * count, count)
            send = lax.dynamic_slice_in_dim(values_in, (1 - up) * count, count)
            values_in = keep + tensor_swap(send.astype(BF16), bit).astype(F32)
            bit *= 2
        return values_in

    def share_of(values_in):
        bit, count = 1, values_in.shape[0]
        while bit < tensor_devices:
            count //= 2
            values_in = lax.dynamic_slice_in_dim(
                values_in, ((third // bit) & 1) * count, count
            )
            bit *= 2
        return values_in

    def share_join(values_in):
        bit = tensor_devices // 2
        while bit:
            got = tensor_swap(values_in, bit)
            up = (third // bit) & 1
            values_in = jnp.where(
                up == 0,
                jnp.concatenate([values_in, got], axis=0),
                jnp.concatenate([got, values_in], axis=0),
            )
            bit //= 2
        return values_in

    partial_out = mm(attended_low, out_weight) + mm(hidden_low, down_weight)
    out_share = (share_of(inputs_f32) + share_sum(partial_out)).astype(BF16)
    block_output = share_join(out_share)

    d_partial = outer_t(d_mixed, qkv_weight) + outer_t(d_gate, gate_weight) + outer_t(d_up, up_weight)
    d_normed = share_sum(d_partial)
    normal_share = share_of(normal)
    grad_share = share_of(out_grad).astype(F32) + norm_back(
        d_normed, normal_share, share_of(inv_dev), gain_f32
    )
    input_grad = share_join(grad_share.astype(BF16)).astype(F32)
    small = jnp.stack([jnp.sum(d_normed * normal_share, axis=0), jnp.sum(d_normed, axis=0)])
    bit, count = devices // 2, width
    while bit:
        count //= 2
        up = (me // bit) & 1
        keep = lax.dynamic_slice_in_dim(small, up * count, count, 1)
        small = keep + swap(lax.dynamic_slice_in_dim(small, (1 - up) * count, count, 1), bit)
        bit //= 2
    bit = 1
    while bit < tensor_devices:
        small = small + tensor_swap(small, bit)
        bit *= 2

    normed_all = jnp.concatenate([normed_chip, normed_far], axis=0)
    grad_all = jnp.concatenate([grad_chip, grad_far], axis=0)

    def columns(values_in, which):
        return lax.dynamic_slice_in_dim(values_in, which * slab, slab, 1)

    normed_keep, normed_send = columns(normed_all, chip), columns(normed_all, chip ^ reduce_bit)
    grad_keep, grad_send = columns(grad_all, chip), columns(grad_all, chip ^ reduce_bit)

    def row_grad(values_in):
        got = reduce_swap(inner(normed_send, values_in).astype(BF16))
        total = inner(normed_keep, values_in) + got.astype(F32)
        keep = lax.dynamic_slice_in_dim(total, core * span_rows, span_rows, 0)
        return keep, swap(lax.dynamic_slice_in_dim(total, (1 - core) * span_rows, span_rows, 0), 1)

    def column_grad(values_in):
        got = reduce_swap(inner(values_in, grad_send).astype(BF16))
        total = inner(values_in, grad_keep) + got.astype(F32)
        keep = lax.dynamic_slice_in_dim(total, core * span_rows, span_rows, 1)
        return keep, swap(lax.dynamic_slice_in_dim(total, (1 - core) * span_rows, span_rows, 1), 1)

    def halves(mine_half, other_half, axis):
        return jnp.concatenate(
            [
                jnp.where(core == 0, mine_half, other_half),
                jnp.where(core == 0, other_half, mine_half),
            ],
            axis=axis,
        )

    gate_grad = whole(*row_grad(d_gate_half), 1)
    up_grad = whole(*row_grad(d_up_half), 1)
    down_grad = whole(*column_grad(hidden_half), 0)
    qkv_grad = halves(*row_grad(d_mixed_half), 1)
    w_out_grad = halves(*column_grad(attended_half), 0)
    return (
        block_output,
        input_grad,
        small[0],
        small[1],
        qkv_grad,
        qkv_bias_grad,
        w_out_grad,
        gate_grad,
        up_grad,
        down_grad,
    )


def solution(mesh):
    in_pairs = mesh.shape["seq"] == 8 and mesh.shape["tensor"] == 4
    return jax.shard_map(
        paired if in_pairs else local,
        mesh=mesh,
        in_specs=(
            P("seq", None),
            P("seq", None),
            P(),
            P(),
            P(None, "tensor"),
            P("tensor"),
            P("tensor", None),
            P(None, "tensor"),
            P(None, "tensor"),
            P("tensor", None),
            P(),
            P(),
        ),
        out_specs=(
            P("seq", None),
            P("seq", None),
            P("seq"),
            P("seq"),
            P("seq", "tensor"),
            P(("tensor", "seq")),
            P("tensor", "seq"),
            P("seq", "tensor"),
            P("seq", "tensor"),
            P("tensor", "seq"),
        ),
        check_vma=False,
    )
```
